256 devices in a mesh: band: 64 (over z, x, core), lev: 4 (over y).
Axes of the slice: x: 4, y: 4, z: 8, core: 2. Of those that a mesh axis runs over, the one named last changes fastest.
Arguments:
- columns: bfloat16 [524288, 274], P(('band', 'lev')), may hold values from -6 to 6
- departures: bfloat16 [4, 2048, 128, 616], P('lev', 'band'), may hold values from -6 to 6
- jacobian: bfloat16 [274, 616], replicated, may hold values from -0.375 to 0.375
- chan_precision: bfloat16 [616, 616], replicated, as said below
- send_rows: int32 [256, 256, 4], P(('band', 'lev')), may hold values from 0 to 2047
- obs_slot: int32 [4, 2048, 128], P('lev', 'band'), may hold values from 0 to 1023
- counts: int32 [4, 2048], P('lev', 'band'), may hold values from 16 to 128, as said below
Outputs:
- column_gradient: float32 [524288, 274], P(('band', 'lev'))
The draws below stay inside these ranges and needn't reach their ends.
Inputs may be any that keep to these rules, and one draw needn't show every extreme that they name: `send_rows`: each entry names a column of the sending device. `obs_slot`: each entry names one of the 1024 slots, ordered by sending device then place. `counts`: each entry is 128 divided by 1, 2, 4 or 8; some entry equals 128. `chan_precision`: symmetric positive definite.
All inputs are finite; a program needn't handle non-finite values.
Results may differ from the reference program's by a relative error of at most 0.0018.
Values may be sent and summed in bfloat16 or wider, within the bound.
No kernel may reach another device: no remote copies, remote signals or barrier semaphores. Data moves between devices by JAX's collectives and lax.ppermute only.
A program may use at most 128 MiB of HBM per device.

```python
import math
import jax
import jax.numpy as jnp
from jax import lax

CHAN = 616
PROF = 274
POS = 128
COLS_DEV = 2048
CAP = 4
LINES_DEV = 32
COLUMNS = 524288
SLOTS = 1024
LINES = 2048
N_LEV = 4
DEVICES = 256


def draw_chan_precision(key, part):
    first_key, second_key = jax.random.split(jax.random.fold_in(key, 17))
    diagonal = jnp.exp(jax.random.uniform(first_key, (CHAN,), jnp.float32, math.log(0.5), math.log(2.0)))
    noise = jax.random.normal(second_key, (CHAN, CHAN), jnp.float32) * (0.35 / (2.0 * math.sqrt(CHAN)))
    symmetric = noise + noise.T
    return (jnp.diag(diagonal) + symmetric).astype(jnp.bfloat16)


def draw_counts(key, part):
    shifts = jax.random.randint(jax.random.fold_in(key, 29), (N_LEV, LINES), 0, 4)
    values = POS // jnp.left_shift(jnp.ones((N_LEV, LINES), jnp.int32), shifts)
    return values.at[0, 0].set(POS).astype(jnp.int32)


def with_ends(array, rng, low, high):
    longest = array.shape.index(max(array.shape))
    spots = []
    for shift in (0, 1):
        where = [jax.random.randint(jax.random.fold_in(rng, axis), (), 0, length) for axis, length in enumerate(array.shape)]
        where[longest] = (where[longest] + shift) % array.shape[longest]
        spots.append(tuple(where))
    return array.at[spots[0]].set(low).at[spots[1]].set(high)


def level_of(stream_key, shape, cuts, least, largest):
    loudness, own = 1.0, jax.random.fold_in(stream_key, 6)
    for dim, shards_of in cuts:
        draws = jnp.exp(jax.random.uniform(jax.random.fold_in(own, dim), (shards_of,), jnp.float32, least / len(cuts), largest / len(cuts)))
        loudness = loudness * jnp.repeat(draws, shape[dim] // shards_of).reshape([-1 if axis == dim else 1 for axis in range(len(shape))])
    return loudness


def scatter_about(own_key, shape, spread, bound, shards=(), kind=jnp.bfloat16):
    result = spread * jax.random.normal(own_key, shape, jnp.float32)
    if shards:
        result = result * level_of(own_key, shape, shards, -0.22, 0.18)
    return jnp.clip(result, -bound, bound).astype(kind)


def setup_inputs(seed: int = 0) -> dict:
    keys = jax.random.split(jax.random.key(seed), 8)
    columns = scatter_about(keys[0], (COLUMNS, PROF), 1.0, 6.0, ((0, 256),))
    departures = scatter_about(keys[1], (N_LEV, LINES, POS, CHAN), 1.0, 6.0, ((0, 4), (1, 64)))
    jacobian = scatter_about(keys[2], (PROF, CHAN), PROF ** -0.5, 0.375)
    chan_precision = draw_chan_precision(jax.random.fold_in(keys[7], 71), 0)
    send_rows = with_ends(jax.random.randint(keys[4], (DEVICES, DEVICES, CAP), 0, COLS_DEV), jax.random.fold_in(keys[4], 1), 0, COLS_DEV - 1).astype(jnp.int32)
    obs_slot = with_ends(jax.random.randint(keys[5], (N_LEV, LINES, POS), 0, SLOTS), jax.random.fold_in(keys[5], 1), 0, SLOTS - 1).astype(jnp.int32)
    counts = draw_counts(jax.random.fold_in(keys[7], 71), 0)
    return {"columns": columns, "departures": departures, "jacobian": jacobian, "chan_precision": chan_precision, "send_rows": send_rows, "obs_slot": obs_slot, "counts": counts}


corr_length = 2.0


def reference(columns, departures, jacobian, chan_precision, send_rows, obs_slot, counts):
    decay_rate = math.exp(-1.0 / corr_length)
    norm_factor = 1.0 / (1.0 - decay_rate * decay_rate)
    positions = jnp.arange(POS, dtype=jnp.int32)

    def make_line(stream, line_index, line_slots, line_deps, line_count):
        observer = (line_index // LINES_DEV) * N_LEV + stream
        source = (line_slots // CAP).astype(jnp.int32)
        place = (line_slots % CAP).astype(jnp.int32)
        global_col = (source * COLS_DEV + send_rows[source, observer, place]).astype(jnp.int32)
        obs_columns = columns[global_col]
        model_equiv = jnp.dot(obs_columns, jacobian, preferred_element_type=jnp.float32)
        valid = positions < line_count
        residual = jnp.where(valid[:, None], model_equiv - line_deps.astype(jnp.float32), 0.0).astype(jnp.bfloat16)
        weighted = jnp.dot(residual, chan_precision, preferred_element_type=jnp.float32)
        return weighted, global_col, valid

    def finish_line(gradient, w_prev, w_cur, w_next, global_col, valid, line_index):
        at_end = (line_index == 0) | (line_index == LINES - 1)
        diag_value = jnp.where(at_end, norm_factor, (1.0 + decay_rate * decay_rate) * norm_factor)
        scaled = diag_value * w_cur - decay_rate * norm_factor * (w_prev + w_next)
        scaled = jnp.where(valid[:, None], scaled, 0.0).astype(jnp.bfloat16)
        obs_adjoint = lax.dot_general(scaled, jacobian, (((1,), (1,)), ((), ())), preferred_element_type=jnp.float32)
        return gradient.at[global_col].add(obs_adjoint)

    gradient = jnp.zeros((COLUMNS, PROF), jnp.float32)
    line_ids = jnp.arange(LINES, dtype=jnp.int32)
    for stream in range(N_LEV):
        def line_step(carry, inputs):
            gradient, w_prev, w_cur, col_cur, valid_cur, index_cur = carry
            line_slots, line_deps, line_count, line_index = inputs
            w_next, col_next, valid_next = make_line(stream, line_index, line_slots, line_deps, line_count)
            gradient = finish_line(gradient, w_prev, w_cur, w_next, col_cur, valid_cur, index_cur)
            return (gradient, w_cur, w_next, col_next, valid_next, line_index), None

        zero_line = jnp.zeros((POS, CHAN), jnp.float32)
        start = (gradient, zero_line, zero_line, jnp.zeros((POS,), jnp.int32), jnp.zeros((POS,), bool), jnp.int32(-1))
        carry, _ = lax.scan(line_step, start, (obs_slot[stream], departures[stream], counts[stream], line_ids))
        gradient, w_prev, w_cur, col_cur, valid_cur, index_cur = carry
        gradient = finish_line(gradient, w_prev, w_cur, zero_line, col_cur, valid_cur, index_cur)
    return gradient
```

```python
import functools
import math

import jax
import jax.numpy as jnp
from jax import lax
from jax.experimental import pallas as pl
from jax.experimental.pallas import tpu as pltpu
from jax.sharding import PartitionSpec as P

corr_length = 2.0
BF, F32 = jnp.bfloat16, jnp.float32
NT = (((1,), (1,)), ((), ()))
VMEM = pl.BlockSpec(memory_space=pltpu.VMEM)
SMEM = pl.BlockSpec(memory_space=pltpu.SMEM)
LIMIT = 58 * 1024 * 1024
MAIN, TAIL_AT, TAIL_STEP, WIRE = 256, 512, 64, 640


def mm(a, b):
    return jnp.dot(a, b, preferred_element_type=F32)


def mm_nt(a, b):
    return lax.dot_general(a, b, NT, preferred_element_type=F32)


def one_hot_t(rows, idx):
    n = idx.shape[1]
    row = lax.broadcasted_iota(jnp.int32, (rows, n), 0)
    return jnp.where(row == idx, 1.0, 0.0).astype(BF)


def store_wire(wire, c, block, prof):
    r, par = c // 2, c % 2
    n = block.shape[1]
    wire[r, :, par * MAIN : (par + 1) * MAIN] = block[:MAIN].T.astype(BF)
    tail = jnp.concatenate([block[MAIN:], jnp.zeros((TAIL_STEP - (prof - MAIN), n), block.dtype)], axis=0)
    return tail


def pack_wire(wire, blocks, prof):
    for r in range(2):
        tails = [store_wire(wire, 2 * r + par, blocks[2 * r + par], prof) for par in range(2)]
        wire[r, :, TAIL_AT:] = jnp.concatenate(tails, axis=0).T.astype(BF)


def unpack_wire(wire, out, prof):
    n = wire.shape[1]
    for r in range(2):
        turned = wire[r].astype(F32).T.astype(BF)
        for par in range(2):
            c = 2 * r + par
            out[0:MAIN, c * n : (c + 1) * n] = turned[par * MAIN : (par + 1) * MAIN]
            at = TAIL_AT + par * TAIL_STEP
            out[MAIN:prof, c * n : (c + 1) * n] = turned[at : at + prof - MAIN]


def send_kernel(cols, plan, wire):
    prof, n_cols = cols.shape
    blocks = [mm(cols[...], one_hot_t(n_cols, plan[c : c + 1, :])) for c in range(4)]
    pack_wire(wire, blocks, prof)


def edge_kernel(wire, slot, valid, dep, jac_t, arrived, resid):
    prof = arrived.shape[0]
    unpack_wire(wire, arrived, prof)
    n_slots = arrived.shape[1]
    n_pos = dep.shape[2]
    last = dep.shape[0] - 1
    for side, line in ((0, 0), (1, last)):
        at = line * n_pos
        hot = one_hot_t(n_slots, slot[:, at : at + n_pos])
        obs = mm(arrived[...], hot).astype(BF)
        model = mm(jac_t[...], obs)
        res = jnp.where(valid[:, at : at + n_pos] > 0, model - dep[line].astype(F32), 0.0)
        resid[:, side * n_pos : (side + 1) * n_pos] = res.astype(BF)


def main_kernel(rf, inner, arrived, slot, valid, dep, jac_t, prec, part, edges, hot_s, w_s, sc_s):
    n_slots = arrived.shape[1]
    n_lines, n_chan, n_pos = dep.shape
    group = 4
    width = group * n_pos

    @pl.loop(0, n_lines // group)
    def _(j):
        at = pl.multiple_of(j * width, width)
        hot = one_hot_t(n_slots, slot[:, pl.ds(at, width)])
        hot_s[:, pl.ds(at, width)] = hot
        obs = mm(arrived[...], hot).astype(BF)
        model = mm(jac_t[...], obs)
        deps = jnp.concatenate([dep[j * group + g] for g in range(group)], axis=1)
        res = jnp.where(valid[:, pl.ds(at, width)] > 0, model - deps.astype(F32), 0.0)
        w_s[:, pl.ds(at, width)] = mm(prec[...], res.astype(BF))

    total = n_lines * n_pos
    zero = jnp.zeros((n_chan, n_pos), BF)
    sc_s[:, 0:n_pos] = zero
    sc_s[:, total - n_pos : total] = zero

    @pl.loop(1, n_lines - 1)
    def _(i):
        at = pl.multiple_of(i * n_pos, n_pos)
        before = w_s[:, pl.ds(at - n_pos, n_pos)]
        after = w_s[:, pl.ds(at + n_pos, n_pos)]
        val = inner * w_s[:, pl.ds(at, n_pos)] - rf * (before + after)
        sc_s[:, pl.ds(at, n_pos)] = jnp.where(valid[:, pl.ds(at, n_pos)] > 0, val, 0.0).astype(BF)

    edges[:, 0 : 2 * n_pos] = w_s[:, 0 : 2 * n_pos]
    edges[:, 2 * n_pos :] = w_s[:, total - 2 * n_pos :]

    step = min(256, n_slots)
    @pl.loop(0, n_slots // step)
    def _(q):
        at = pl.multiple_of(q * step, step)
        part[:, pl.ds(at, step)] = mm_nt(sc_s[...], hot_s[pl.ds(at, step), :])


def finish_kernel(rf, diag, halo, edges, slot, valid, part, jac, prec, wire):
    prof = jac.shape[0]
    n_slots = part.shape[1]
    n_pos = halo.shape[1] // 2
    total = slot.shape[1]
    outer = mm(prec[...], halo[...])
    ends = []
    for side, line_at in ((0, 0), (1, total - n_pos)):
        own = edges[:, 3 * side * n_pos : (3 * side + 1) * n_pos]
        inside = edges[:, (1 + side) * n_pos : (2 + side) * n_pos]
        beyond = outer[:, side * n_pos : (side + 1) * n_pos]
        val = diag[side] * own - rf * (inside + beyond)
        ends.append(jnp.where(valid[:, line_at : line_at + n_pos] > 0, val, 0.0).astype(BF))
    scaled = jnp.concatenate(ends, axis=1)
    idx = jnp.concatenate([slot[:, 0:n_pos], slot[:, total - n_pos :]], axis=1)
    blocks = []
    step = n_slots // 4
    for c in range(4):
        row = lax.broadcasted_iota(jnp.int32, (step, 2 * n_pos), 0) + c * step
        hot = jnp.where(row == idx, 1.0, 0.0).astype(BF)
        sums = part[:, c * step : (c + 1) * step] + mm_nt(scaled, hot)
        high = sums.astype(BF)
        low = (sums - high.astype(F32)).astype(BF)
        blocks.append(mm(jac[...], high) + mm(jac[...], low))
    pack_wire(wire, blocks, prof)


def collect_kernel(wire, plan, grad, back):
    prof = back.shape[0]
    unpack_wire(wire, back, prof)
    n = plan.shape[1]
    step = min(512, grad.shape[1])

    @pl.loop(0, grad.shape[1] // step)
    def _(q):
        at = pl.multiple_of(q * step, step)
        hots = []
        for c in range(4):
            row = lax.broadcasted_iota(jnp.int32, (step, n), 0) + at
            hots.append(jnp.where(row == plan[c : c + 1, :], 1.0, 0.0).astype(BF))
        grad[:, pl.ds(at, step)] = mm_nt(back[...], jnp.concatenate(hots, axis=1))


def call(body, outs, n_in, scratch=(), smem=()):
    specs = [SMEM if i in smem else VMEM for i in range(n_in)]
    return pl.pallas_call(
        body,
        out_shape=outs,
        in_specs=specs,
        out_specs=[VMEM] * len(outs),
        scratch_shapes=list(scratch),
        compiler_params=pltpu.CompilerParams(vmem_limit_bytes=LIMIT),
    )


def on_device(columns, departures, jacobian, chan_precision, send_rows, obs_slot, counts):
    decay = math.exp(-1.0 / corr_length)
    norm = 1.0 / (1.0 - decay * decay)
    rf, inner = decay * norm, (1.0 + decay * decay) * norm
    n_band = lax.axis_size("band")
    n_dev = n_band * lax.axis_size("lev")
    n_cols, prof = columns.shape
    _, n_lines, n_pos, n_chan = departures.shape
    total = n_lines * n_pos
    depth = send_rows.shape[2]
    n_slots = n_dev * depth
    sds = jax.ShapeDtypeStruct

    plan = send_rows[0].T
    jac_t = jacobian.T
    dep = departures[0].transpose(0, 2, 1)
    slots = obs_slot[0].reshape(1, total)
    slots = (slots % depth) * n_dev + slots // depth
    valid = jnp.arange(n_pos, dtype=jnp.int32)[None, :] < counts[0][:, None]
    valid = valid.astype(jnp.int32).reshape(1, total)

    wire_shape = sds((2, n_dev, WIRE), BF)

    def exchange(wire):
        sent = wire.transpose(1, 0, 2)
        got = lax.all_to_all(sent, ("band", "lev"), split_axis=0, concat_axis=0, tiled=True)
        return got.transpose(1, 0, 2)

    (wire,) = call(send_kernel, [wire_shape], 2)(columns.T, plan)
    got = exchange(wire)
    arrived, resid = call(
        edge_kernel, [sds((prof, n_slots), BF), sds((n_chan, 2 * n_pos), BF)], 5
    )(got, slots, valid, dep, jac_t)
    ends = n_band - 1
    from_before = lax.ppermute(resid[:, n_pos:], "band", [(i, i + 1) for i in range(ends)])
    from_after = lax.ppermute(resid[:, :n_pos], "band", [(i + 1, i) for i in range(ends)])
    part, edges = call(
        functools.partial(main_kernel, rf, inner),
        [sds((n_chan, n_slots), F32), sds((n_chan, 4 * n_pos), F32)],
        6,
        scratch=[
            pltpu.VMEM((n_slots, total), BF),
            pltpu.VMEM((n_chan, total), F32),
            pltpu.VMEM((n_chan, total), BF),
        ],
    )(arrived, slots, valid, dep, jac_t, chan_precision)
    halo = jnp.concatenate([from_before, from_after], axis=1)
    band = lax.axis_index("band")
    diag = jnp.stack([jnp.where(band == 0, norm, inner), jnp.where(band == ends, norm, inner)]).astype(F32)
    (wire,) = call(functools.partial(finish_kernel, rf), [wire_shape], 8, smem=(0,))(
        diag, halo, edges, slots, valid, part, jacobian, chan_precision
    )
    back = exchange(wire)
    (grad,) = call(
        collect_kernel, [sds((prof, n_cols), F32)], 2, scratch=[pltpu.VMEM((prof, n_slots), BF)]
    )(back, plan)
    return grad.T


def solution(mesh):
    placed = (
        P(("band", "lev"), None),
        P("lev", "band", None, None),
        P(),
        P(),
        P(("band", "lev"), None, None),
        P("lev", "band", None),
        P("lev", "band"),
    )
    return jax.shard_map(
        on_device, mesh=mesh, in_specs=placed, out_specs=P(("band", "lev"), None), check_vma=False
    )
```

```python
import functools
import math

import jax
import jax.numpy as jnp
from jax import lax
from jax.experimental import pallas as pl
from jax.experimental.pallas import tpu as pltpu
from jax.sharding import PartitionSpec as P

corr_length = 2.0
BF, F32 = jnp.bfloat16, jnp.float32
NT = (((1,), (1,)), ((), ()))
VMEM = pl.BlockSpec(memory_space=pltpu.VMEM)
SMEM = pl.BlockSpec(memory_space=pltpu.SMEM)
HBM = pl.BlockSpec(memory_space=pltpu.HBM)
MIB = 1024 * 1024
MAIN, TAIL_AT, TAIL_STEP, WIRE = 256, 512, 64, 640


def mm(a, b):
    return jnp.dot(a, b, preferred_element_type=F32)


def mm_nt(a, b):
    return lax.dot_general(a, b, NT, preferred_element_type=F32)


def one_hot_t(rows, idx):
    n = idx.shape[1]
    row = lax.broadcasted_iota(jnp.int32, (rows, n), 0)
    return jnp.where(row == idx, 1.0, 0.0).astype(BF)


def store_wire(wire, c, block, prof):
    r, par = c // 2, c % 2
    n = block.shape[1]
    wire[r, :, par * MAIN : (par + 1) * MAIN] = block[:MAIN].T.astype(BF)
    tail = jnp.concatenate([block[MAIN:], jnp.zeros((TAIL_STEP - (prof - MAIN), n), block.dtype)], axis=0)
    return tail


def pack_wire(wire, blocks, prof):
    for r in range(2):
        tails = [store_wire(wire, 2 * r + par, blocks[2 * r + par], prof) for par in range(2)]
        wire[r, :, TAIL_AT:] = jnp.concatenate(tails, axis=0).T.astype(BF)


def unpack_wire(wire, out, prof):
    n = wire.shape[1]
    for r in range(2):
        turned = wire[r].astype(F32).T.astype(BF)
        for par in range(2):
            c = 2 * r + par
            out[0:MAIN, c * n : (c + 1) * n] = turned[par * MAIN : (par + 1) * MAIN]
            at = TAIL_AT + par * TAIL_STEP
            out[MAIN:prof, c * n : (c + 1) * n] = turned[at : at + prof - MAIN]


def send_kernel(cols_in, plan, wire, hot, cols, sem):
    prof, n_cols = cols.shape
    copy = pltpu.make_async_copy(cols_in, cols, sem)
    copy.start()
    n = plan.shape[1]
    for c in range(4):
        hot[:, c * n : (c + 1) * n] = one_hot_t(n_cols, plan[c : c + 1, :])
    copy.wait()
    blocks = [mm(cols[...], hot[:, c * n : (c + 1) * n]) for c in range(4)]
    pack_wire(wire, blocks, prof)


def hot_kernel(slot, hot):
    width = 512

    @pl.loop(0, hot.shape[1] // width)
    def _(j):
        at = pl.multiple_of(j * width, width)
        hot[:, pl.ds(at, width)] = one_hot_t(hot.shape[0], slot[:, pl.ds(at, width)])


def hot_plan_kernel(plan, hot):
    n = plan.shape[1]
    for c in range(4):
        hot[:, c * n : (c + 1) * n] = one_hot_t(hot.shape[0], plan[c : c + 1, :])


def edge_kernel(wire, slot, valid, dep, jac_t, arrived, first, last, deps, sems):
    copies = [
        pltpu.make_async_copy(dep.at[line], deps.at[k], sems.at[k]) for k, line in enumerate((0, dep.shape[0] - 1))
    ]
    for copy in copies:
        copy.start()
    prof, n_slots = arrived.shape
    unpack_wire(wire, arrived, prof)
    n_pos = dep.shape[2]
    end = slot.shape[1] - n_pos
    idx = jnp.concatenate([slot[:, :n_pos], slot[:, end:]], axis=1)
    obs = mm(arrived[...], one_hot_t(n_slots, idx)).astype(BF)
    model = mm(jac_t[...], obs)
    for k, at, out in ((0, 0, first), (1, end, last)):
        copies[k].wait()
        res = model[:, k * n_pos : (k + 1) * n_pos] - deps[k].astype(F32)
        out[...] = jnp.where(valid[:, at : at + n_pos] > 0, res, 0.0).astype(BF)


def main_kernel(rf, inner, arrived, hot_in, valid, dep, jac_t, prec, first, last, part, edges, *scratch):
    w_s, sc_s, deps, hot, sems = scratch[:5]
    obs_s, res_s = scratch[5:7], scratch[7:]
    n_slots = arrived.shape[1]
    n_lines, n_chan, n_pos = dep.shape
    total = n_lines * n_pos
    groups = []
    line = 1
    while line < n_lines - 1:
        size = min(4, n_lines - 1 - line)
        groups.append((line, size))
        line += size
    copies = []
    for g, (line, size) in enumerate(groups):
        span, lanes = pl.ds(line, size), pl.ds(line * n_pos, size * n_pos)
        pair = (
            pltpu.make_async_copy(hot_in.at[:, lanes], hot.at[:, lanes], sems.at[0, g]),
            pltpu.make_async_copy(dep.at[span], deps.at[span], sems.at[1, g]),
        )
        for copy in pair:
            copy.start()
        copies.append(pair)

    def gather(g):
        line, size = groups[g]
        lanes = slice(line * n_pos, (line + size) * n_pos)
        copies[g][0].wait()
        obs_s[g % 2][:, : size * n_pos] = mm(arrived[...], hot[:, lanes]).astype(BF)

    def residual(g):
        line, size = groups[g]
        lanes = slice(line * n_pos, (line + size) * n_pos)
        model = mm(jac_t[...], obs_s[g % 2][:, : size * n_pos])
        copies[g][1].wait()
        own = jnp.concatenate([deps[line + k] for k in range(size)], axis=1)
        res = jnp.where(valid[:, lanes] > 0, model - own.astype(F32), 0.0)
        res_s[g % 2][:, : size * n_pos] = res.astype(BF)

    def weigh(g):
        line, size = groups[g]
        w_s[:, line * n_pos : (line + size) * n_pos] = mm(prec[...], res_s[g % 2][:, : size * n_pos])

    def scale(i):
        at = i * n_pos
        beside = w_s[:, at - n_pos : at] + w_s[:, at + n_pos : at + 2 * n_pos]
        val = inner * w_s[:, at : at + n_pos] - rf * beside
        sc_s[:, at : at + n_pos] = jnp.where(valid[:, at : at + n_pos] > 0, val, 0.0).astype(BF)

    outer = mm(prec[...], jnp.concatenate([first[...], last[...]], axis=1))
    w_s[:, :n_pos] = outer[:, :n_pos]
    w_s[:, total - n_pos :] = outer[:, n_pos:]
    done = 1
    count = len(groups)
    for t in range(count + 3):
        if t < count:
            gather(t)
        if 0 <= t - 1 < count:
            residual(t - 1)
        if 0 <= t - 2 < count:
            weigh(t - 2)
        if 0 <= t - 3 < count:
            line, size = groups[t - 3]
            stop = n_lines - 1 if t - 3 == count - 1 else line + size - 1
            while done < stop:
                scale(done)
                done += 1

    edges[:, : 2 * n_pos] = w_s[:, : 2 * n_pos]
    edges[:, 2 * n_pos :] = w_s[:, total - 2 * n_pos :]
    lanes = slice(n_pos, total - n_pos)
    step = min(256, n_slots)

    @pl.loop(0, n_slots // step)
    def _(q):
        at = pl.multiple_of(q * step, step)
        part[:, pl.ds(at, step)] = mm_nt(sc_s[:, lanes], hot[pl.ds(at, step), lanes])


def finish_kernel(rf, norm, inner, n_band, band, before, after, edges, slot, valid, part, jac, prec, wire):
    prof = jac.shape[0]
    n_slots = part.shape[1]
    n_pos = before.shape[1]
    total = slot.shape[1]
    outer = mm(prec[...], jnp.concatenate([before[...], after[...]], axis=1))
    ends = []
    for side, line_at, bound in ((0, 0, 0), (1, total - n_pos, n_band - 1)):
        own = edges[:, 3 * side * n_pos : (3 * side + 1) * n_pos]
        inside = edges[:, (1 + side) * n_pos : (2 + side) * n_pos]
        beyond = outer[:, side * n_pos : (side + 1) * n_pos]
        diag = jnp.where(band[0] == bound, norm, inner).astype(F32)
        val = diag * own - rf * (inside + beyond)
        ends.append(jnp.where(valid[:, line_at : line_at + n_pos] > 0, val, 0.0).astype(BF))
    scaled = jnp.concatenate(ends, axis=1)
    idx = jnp.concatenate([slot[:, 0:n_pos], slot[:, total - n_pos :]], axis=1)
    blocks = []
    step = n_slots // 4
    for c in range(4):
        row = lax.broadcasted_iota(jnp.int32, (step, 2 * n_pos), 0) + c * step
        hot = jnp.where(row == idx, 1.0, 0.0).astype(BF)
        sums = part[:, c * step : (c + 1) * step] + mm_nt(scaled, hot)
        high = sums.astype(BF)
        low = (sums - high.astype(F32)).astype(BF)
        blocks.append(mm(jac[...], high) + mm(jac[...], low))
    pack_wire(wire, blocks, prof)


def collect_kernel(wire, hot_in, grad, back, hot, out, sems):
    prof = back.shape[0]
    n_steps, step = out.shape[0], out.shape[2]
    copies = []
    for q in range(n_steps):
        rows = pl.ds(q * step, step)
        pair = (
            pltpu.make_async_copy(hot_in.at[rows], hot.at[rows], sems.at[0, q]),
            pltpu.make_async_copy(out.at[q], grad.at[:, rows], sems.at[1, q]),
        )
        pair[0].start()
        copies.append(pair)
    unpack_wire(wire, back, prof)
    for q in range(n_steps):
        copies[q][0].wait()
        out[q] = mm_nt(back[...], hot[q * step : (q + 1) * step, :])
        copies[q][1].start()
    for q in range(n_steps):
        copies[q][1].wait()


def call(body, outs, in_specs, limit, flops=0, scratch=(), out_specs=None):
    return pl.pallas_call(
        body,
        out_shape=outs,
        in_specs=in_specs,
        out_specs=out_specs or [VMEM] * len(outs),
        scratch_shapes=list(scratch),
        compiler_params=pltpu.CompilerParams(vmem_limit_bytes=int(limit * MIB)),
        cost_estimate=pl.CostEstimate(flops=flops, bytes_accessed=8 * MIB, transcendentals=0),
    )


def on_device(columns, departures, jacobian, chan_precision, send_rows, obs_slot, counts):
    decay = math.exp(-1.0 / corr_length)
    norm = 1.0 / (1.0 - decay * decay)
    rf, inner = decay * norm, (1.0 + decay * decay) * norm
    n_band = lax.axis_size("band")
    n_dev = n_band * lax.axis_size("lev")
    n_cols, prof = columns.shape
    _, n_lines, n_pos, n_chan = departures.shape
    total = n_lines * n_pos
    depth = send_rows.shape[2]
    n_slots = n_dev * depth
    sds = jax.ShapeDtypeStruct

    plan = send_rows[0].T
    jac_t = jacobian.T
    dep = departures[0].transpose(0, 2, 1)
    slots = obs_slot[0].reshape(1, total)
    slots = (slots % depth) * n_dev + slots // depth
    valid = jnp.arange(n_pos, dtype=jnp.int32)[None, :] < counts[0][:, None]
    valid = valid.astype(jnp.int32).reshape(1, total)

    wire_shape = sds((2, n_dev, WIRE), BF)

    def exchange(wire):
        sent = wire.transpose(1, 0, 2)
        got = lax.all_to_all(sent, ("band", "lev"), split_axis=0, concat_axis=0, tiled=True)
        return got.transpose(1, 0, 2)

    hot_shape = sds((n_cols, n_slots), BF)
    (wire,) = call(
        send_kernel,
        [wire_shape],
        [HBM, VMEM],
        62.9,
        2**31,
        scratch=[pltpu.VMEM((n_cols, n_slots), BF), pltpu.VMEM((prof, n_cols), BF), pltpu.SemaphoreType.DMA],
    )(columns.T, plan)
    got = exchange(wire)
    (hot,) = call(hot_kernel, [sds((n_slots, total), BF)], [VMEM], 60, 2**32)(slots)
    line_shape = sds((n_chan, n_pos), BF)
    arrived, first, last = call(
        edge_kernel,
        [sds((prof, n_slots), BF), line_shape, line_shape],
        [VMEM] * 3 + [HBM, VMEM],
        60,
        2**30,
        scratch=[pltpu.VMEM((2, n_chan, n_pos), BF), pltpu.SemaphoreType.DMA((2,))],
    )(got, slots, valid, dep, jac_t)
    ends = n_band - 1
    before = lax.ppermute(last, "band", [(i, i + 1) for i in range(ends)])
    after = lax.ppermute(first, "band", [(i + 1, i) for i in range(ends)])
    part, edges = call(
        functools.partial(main_kernel, rf, inner),
        [sds((n_chan, n_slots), F32), sds((n_chan, 4 * n_pos), F32)],
        [VMEM, HBM, VMEM, HBM] + [VMEM] * 4,
        60,
        2**34,
        scratch=[
            pltpu.VMEM((n_chan, total), F32),
            pltpu.VMEM((n_chan, total), BF),
            pltpu.VMEM((n_lines, n_chan, n_pos), BF),
            pltpu.VMEM((n_slots, total), BF),
            pltpu.SemaphoreType.DMA((2, n_lines)),
        ]
        + [pltpu.VMEM((prof, 4 * n_pos), BF)] * 2
        + [pltpu.VMEM((n_chan, 4 * n_pos), BF)] * 2,
    )(arrived, hot, valid, dep, jac_t, chan_precision, first, last)
    band = lax.axis_index("band").reshape(1)
    (wire,) = call(
        functools.partial(finish_kernel, rf, norm, inner, n_band),
        [wire_shape],
        [SMEM] + [VMEM] * 8,
        16,
        2**31,
    )(band, before, after, edges, slots, valid, part, jacobian, chan_precision)
    wire, late_plan = lax.optimization_barrier((wire, plan))
    back = exchange(wire)
    (hot_cols,) = call(hot_plan_kernel, [hot_shape], [VMEM], 60, 2**32)(late_plan)
    (grad,) = call(
        collect_kernel,
        [sds((prof, n_cols), F32)],
        [VMEM, HBM],
        61,
        2**31,
        scratch=[
            pltpu.VMEM((prof, n_slots), BF),
            pltpu.VMEM((n_cols, n_slots), BF),
            pltpu.VMEM((4, prof, n_cols // 4), F32),
            pltpu.SemaphoreType.DMA((2, 4)),
        ],
        out_specs=[HBM],
    )(back, hot_cols)
    return grad.T


def solution(mesh):
    placed = (
        P(("band", "lev"), None),
        P("lev", "band", None, None),
        P(),
        P(),
        P(("band", "lev"), None, None),
        P("lev", "band", None),
        P("lev", "band"),
    )
    return jax.shard_map(
        on_device, mesh=mesh, in_specs=placed, out_specs=P(("band", "lev"), None), check_vma=False
    )
```

```python
import functools
import math

import jax
import jax.numpy as jnp
from jax import lax
from jax.experimental import pallas as pl
from jax.experimental.pallas import tpu as pltpu
from jax.sharding import PartitionSpec as P

corr_length = 2.0
BF, F32 = jnp.bfloat16, jnp.float32
NT = (((1,), (1,)), ((), ()))
VMEM = pl.BlockSpec(memory_space=pltpu.VMEM)
SMEM = pl.BlockSpec(memory_space=pltpu.SMEM)
HBM = pl.BlockSpec(memory_space=pltpu.HBM)
MIB = 1024 * 1024
LIMITS = (16, 60, 60, 60, 16)
GROUP = 4
MAIN, TAIL_AT, TAIL_STEP, WIRE = 256, 512, 64, 640


def mm(a, b):
    return jnp.dot(a, b, preferred_element_type=F32)


def mm_nt(a, b):
    return lax.dot_general(a, b, NT, preferred_element_type=F32)


def write_hot(out, first_col, idx, base=0):
    n = idx.shape[1]
    row = lax.broadcasted_iota(jnp.int32, (16, n), 0) + base
    gap = (jnp.broadcast_to(idx, (16, n)) - row).astype(jnp.int16)
    one, zero = jnp.ones((16, n), BF), jnp.zeros((16, n), BF)
    for r in range(0, out.shape[0], 16):
        out[r : r + 16, pl.ds(first_col, n)] = jnp.where(gap == jnp.int16(r), one, zero)


def pack_wire(wire, r, blocks, prof):
    n = blocks[0].shape[1]
    tails = []
    for par, block in enumerate(blocks):
        wire[r, :, par * MAIN : (par + 1) * MAIN] = block[:MAIN].T.astype(BF)
        fill = jnp.zeros((TAIL_STEP - (prof - MAIN), n), block.dtype)
        tails.extend([block[MAIN:], fill])
    wire[r, :, TAIL_AT:] = jnp.concatenate(tails, axis=0).T.astype(BF)


def unpack_wire(wire, out, prof):
    n = wire.shape[1]
    for r in range(2):
        turned = wire[r].astype(F32).T.astype(BF)
        for par in range(2):
            c = 2 * r + par
            out[0:MAIN, c * n : (c + 1) * n] = turned[par * MAIN : (par + 1) * MAIN]
            at = TAIL_AT + par * TAIL_STEP
            out[MAIN:prof, c * n : (c + 1) * n] = turned[at : at + prof - MAIN]


def send_kernel(cols_in, plan, wire, hot, cols, sem):
    prof, n_cols = cols.shape
    copy = pltpu.make_async_copy(cols_in, cols, sem)
    copy.start()
    n = plan.shape[1]
    for c in range(4):
        write_hot(hot, c * n, plan[c : c + 1, :])
    copy.wait()
    for r in range(2):
        blocks = [mm(cols[...], hot[:, c * n : (c + 1) * n]) for c in (2 * r, 2 * r + 1)]
        pack_wire(wire, r, blocks, prof)


def hot_kernel(slot, hot):
    width = 512

    @pl.loop(0, hot.shape[1] // width)
    def _(j):
        at = pl.multiple_of(j * width, width)
        write_hot(hot, at, slot[:, pl.ds(at, width)])


def edge_kernel(wire, slot, valid, dep, jac_t, arrived, first, last, deps, hot, sems):
    copies = [
        pltpu.make_async_copy(dep.at[line], deps.at[k], sems.at[k]) for k, line in enumerate((0, dep.shape[0] - 1))
    ]
    for copy in copies:
        copy.start()
    prof = arrived.shape[0]
    unpack_wire(wire, arrived, prof)
    n_pos = dep.shape[2]
    end = slot.shape[1] - n_pos
    write_hot(hot, 0, jnp.concatenate([slot[:, :n_pos], slot[:, end:]], axis=1))
    obs = mm(arrived[...], hot[...]).astype(BF)
    model = mm(jac_t[...], obs)
    for k, at, out in ((0, 0, first), (1, end, last)):
        copies[k].wait()
        res = model[:, k * n_pos : (k + 1) * n_pos] - deps[k].astype(F32)
        out[...] = jnp.where(valid[:, at : at + n_pos] > 0, res, 0.0).astype(BF)


def main_kernel(rf, inner, arrived_in, hot_in, valid, dep, jac_in, prec_in, part_out, edges_out, *scratch):
    arrived, jac_t, prec, deps, hot, obs_s, res_s, w_s, sc_s, part, in_sem, group_sem, out_sem = scratch
    n_slots = arrived.shape[1]
    n_lines, n_chan, n_pos = dep.shape
    total = n_lines * n_pos
    size = GROUP
    width = size * n_pos
    count = n_lines // size

    def hot_copy(g):
        lanes = pl.ds(pl.multiple_of(g * width, width), width)
        return pltpu.make_async_copy(hot_in.at[:, lanes], hot.at[:, lanes], group_sem.at[0, g])

    def dep_copy(g):
        span = pl.ds(g * size, size)
        return pltpu.make_async_copy(dep.at[span], deps.at[span], group_sem.at[1, g])

    whole = [
        pltpu.make_async_copy(src, dst, in_sem.at[k])
        for k, (src, dst) in enumerate(((arrived_in, arrived), (jac_in, jac_t), (prec_in, prec)))
    ]
    for copy in whole:
        copy.start()
    for g in range(count):
        hot_copy(g).start()
        dep_copy(g).start()
    for copy in whole:
        copy.wait()

    @pl.loop(0, count)
    def _(g):
        hot_copy(g).wait()
        dep_copy(g).wait()
        lanes = pl.ds(pl.multiple_of(g * width, width), width)
        obs_s[...] = mm(arrived[...], hot[:, lanes]).astype(BF)
        model = mm(jac_t[...], obs_s[...])
        own = jnp.concatenate([deps[g * size + k] for k in range(size)], axis=1)
        res_s[...] = jnp.where(valid[:, lanes] > 0, model - own.astype(F32), 0.0).astype(BF)
        w_s[:, lanes] = rf * mm(prec[...], res_s[...])

    sides = [
        pltpu.make_async_copy(w_s.at[:, pl.ds(at, 2 * n_pos)], edges_out.at[:, pl.ds(to, 2 * n_pos)], out_sem.at[4 + k])
        for k, (at, to) in enumerate(((0, 0), (total - 2 * n_pos, 2 * n_pos)))
    ]
    for copy in sides:
        copy.start()

    def scale(rows):
        before, here = w_s[rows, 0:n_pos], w_s[rows, n_pos : 2 * n_pos]
        for i in range(1, n_lines - 1):
            after = w_s[rows, (i + 1) * n_pos : (i + 2) * n_pos]
            sc_s[rows, i * n_pos : (i + 1) * n_pos] = ((inner / rf) * here - (before + after)).astype(BF)
            before, here = here, after

    @pl.loop(0, n_chan // 16)
    def _(c):
        scale(pl.ds(pl.multiple_of(c * 16, 16), 16))

    if n_chan % 16:
        scale(pl.ds(n_chan // 16 * 16, n_chan % 16))

    inside = slice(n_pos, total - n_pos)
    step = n_slots // 4

    def part_copy(q):
        lanes = pl.ds(pl.multiple_of(q * step, step), step)
        return pltpu.make_async_copy(part.at[:, lanes], part_out.at[:, lanes], out_sem.at[q])

    @pl.loop(0, 4)
    def _(q):
        at = pl.multiple_of(q * step, step)
        part[:, pl.ds(at, step)] = mm_nt(sc_s[:, inside], hot[pl.ds(at, step), inside])
        part_copy(q).start()

    for copy in sides:
        copy.wait()
    for q in range(4):
        part_copy(q).wait()


def finish_kernel(rf, norm, inner, n_band, band, before, after, edges_in, slot, part_in, jac, prec, wire, *scratch):
    edges, part, sems = scratch
    prof = jac.shape[0]
    n_slots = part.shape[1]
    n_pos = before.shape[1]
    total = slot.shape[1]
    step = n_slots // 4
    copies = [pltpu.make_async_copy(edges_in, edges, sems.at[4])]
    for c in range(4):
        lanes = pl.ds(c * step, step)
        copies.append(pltpu.make_async_copy(part_in.at[:, lanes], part.at[:, lanes], sems.at[c]))
    for copy in copies:
        copy.start()
    outer = rf * mm(prec[...], jnp.concatenate([before[...], after[...]], axis=1))
    copies[0].wait()
    ends = []
    for side, bound in ((0, 0), (1, n_band - 1)):
        own = edges[:, 3 * side * n_pos : (3 * side + 1) * n_pos]
        inside = edges[:, (1 + side) * n_pos : (2 + side) * n_pos]
        beyond = outer[:, side * n_pos : (side + 1) * n_pos]
        ratio = jnp.where(band[0] == bound, norm / rf, inner / rf).astype(F32)
        ends.append((ratio * own - (inside + beyond)).astype(BF))
    scaled = jnp.concatenate(ends, axis=1)
    idx = jnp.concatenate([slot[:, 0:n_pos], slot[:, total - n_pos :]], axis=1)
    for copy in copies[1:]:
        copy.wait()
    for r in range(2):
        blocks = []
        for c in (2 * r, 2 * r + 1):
            row = lax.broadcasted_iota(jnp.int32, (step, 2 * n_pos), 0) + c * step
            hot = jnp.where(row == idx, 1.0, 0.0).astype(BF)
            sums = part[:, c * step : (c + 1) * step] + mm_nt(scaled, hot)
            high = sums.astype(BF)
            low = (sums - high.astype(F32)).astype(BF)
            blocks.append(mm(jac[...], high) + mm(jac[...], low))
        pack_wire(wire, r, blocks, prof)


def collect_kernel(wire, plan, grad, back, hot, out, sems):
    prof = back.shape[0]
    n_steps, step = out.shape[0], out.shape[2]
    n = plan.shape[1]
    unpack_wire(wire, back, prof)
    copies = []
    for q in range(n_steps):
        for c in range(4):
            write_hot(hot.at[q], c * n, plan[c : c + 1, :], q * step)
        out[q] = mm_nt(back[...], hot[q])
        copies.append(pltpu.make_async_copy(out.at[q], grad.at[:, pl.ds(q * step, step)], sems.at[q]))
        copies[q].start()
    for copy in copies:
        copy.wait()


def call(body, outs, in_specs, limit, flops=0, scratch=(), out_specs=None):
    return pl.pallas_call(
        body,
        out_shape=outs,
        in_specs=in_specs,
        out_specs=out_specs or [VMEM] * len(outs),
        scratch_shapes=list(scratch),
        compiler_params=pltpu.CompilerParams(vmem_limit_bytes=int(limit * MIB)),
        cost_estimate=pl.CostEstimate(flops=flops, bytes_accessed=8 * MIB, transcendentals=0),
    )


def on_device(columns, departures, jacobian, chan_precision, send_rows, obs_slot, counts):
    decay = math.exp(-1.0 / corr_length)
    norm = 1.0 / (1.0 - decay * decay)
    rf, inner = decay * norm, (1.0 + decay * decay) * norm
    n_band = lax.axis_size("band")
    n_dev = n_band * lax.axis_size("lev")
    n_cols, prof = columns.shape
    _, n_lines, n_pos, n_chan = departures.shape
    total = n_lines * n_pos
    depth = send_rows.shape[2]
    n_slots = n_dev * depth
    sds = jax.ShapeDtypeStruct

    plan = send_rows[0].T
    jac_t = jacobian.T
    dep = departures[0].transpose(0, 2, 1)
    valid = jnp.arange(n_pos, dtype=jnp.int32)[None, :] < counts[0][:, None]
    slots = (obs_slot[0] % depth) * n_dev + obs_slot[0] // depth
    slots = jnp.where(valid, slots, -1).reshape(1, total)
    valid = valid.astype(jnp.int32).reshape(1, total)

    wire_shape = sds((2, n_dev, WIRE), BF)

    def exchange(wire):
        sent = wire.transpose(1, 0, 2)
        got = lax.all_to_all(sent, ("band", "lev"), split_axis=0, concat_axis=0, tiled=True)
        return got.transpose(1, 0, 2)

    dma = pltpu.SemaphoreType.DMA
    vm = pltpu.VMEM
    (wire,) = call(
        send_kernel,
        [wire_shape],
        [HBM, VMEM],
        LIMITS[0],
        2**31,
        scratch=[vm((n_cols, n_slots), BF), vm((prof, n_cols), BF), dma],
    )(columns.T, plan)
    got = exchange(wire)
    (hot,) = call(hot_kernel, [sds((n_slots, total), BF)], [VMEM], 60, 2**32)(slots)
    line_shape = sds((n_chan, n_pos), BF)
    arrived, first, last = call(
        edge_kernel,
        [sds((prof, n_slots), BF), line_shape, line_shape],
        [VMEM] * 3 + [HBM, VMEM],
        LIMITS[1],
        2**30,
        scratch=[vm((2, n_chan, n_pos), BF), vm((n_slots, 2 * n_pos), BF), dma((2,))],
    )(got, slots, valid, dep, jac_t)
    ends = n_band - 1
    before = lax.ppermute(last, "band", [(i, i + 1) for i in range(ends)])
    after = lax.ppermute(first, "band", [(i + 1, i) for i in range(ends)])
    part, edges = call(
        functools.partial(main_kernel, rf, inner),
        [sds((n_chan, n_slots), F32), sds((n_chan, 4 * n_pos), F32)],
        [HBM, HBM, VMEM, HBM, HBM, HBM],
        LIMITS[2],
        2**34,
        scratch=[
            vm((prof, n_slots), BF),
            vm((n_chan, prof), BF),
            vm((n_chan, n_chan), BF),
            vm((n_lines, n_chan, n_pos), BF),
            vm((n_slots, total), BF),
            vm((prof, GROUP * n_pos), BF),
            vm((n_chan, GROUP * n_pos), BF),
            vm((n_chan, total), F32),
            vm((n_chan, total), BF),
            vm((n_chan, n_slots), F32),
            dma((3,)),
            dma((2, n_lines // GROUP)),
            dma((6,)),
        ],
        out_specs=[HBM] * 2,
    )(arrived, hot, valid, dep, jac_t, chan_precision)
    band = lax.axis_index("band").reshape(1)
    (wire,) = call(
        functools.partial(finish_kernel, rf, norm, inner, n_band),
        [wire_shape],
        [SMEM, VMEM, VMEM, HBM, VMEM, HBM, VMEM, VMEM],
        LIMITS[3],
        2**31,
        scratch=[vm((n_chan, 4 * n_pos), F32), vm((n_chan, n_slots), F32), dma((5,))],
    )(band, before, after, edges, slots, part, jacobian, chan_precision)
    back = exchange(wire)
    (grad,) = call(
        collect_kernel,
        [sds((prof, n_cols), F32)],
        [VMEM, VMEM],
        LIMITS[4],
        2**31,
        scratch=[
            vm((prof, n_slots), BF),
            vm((4, n_cols // 4, n_slots), BF),
            vm((4, prof, n_cols // 4), F32),
            dma((4,)),
        ],
        out_specs=[HBM],
    )(back, plan)
    return grad.T


def solution(mesh):
    placed = (
        P(("band", "lev"), None),
        P("lev", "band", None, None),
        P(),
        P(),
        P(("band", "lev"), None, None),
        P("lev", "band", None),
        P("lev", "band"),
    )
    return jax.shard_map(
        on_device, mesh=mesh, in_specs=placed, out_specs=P(("band", "lev"), None), check_vma=False
    )
```

```python
import functools
import math

import jax
import jax.numpy as jnp
from jax import lax
from jax.experimental import pallas as pl
from jax.experimental.pallas import tpu as pltpu
from jax.sharding import PartitionSpec as P

corr_length = 2.0
BF, F32 = jnp.bfloat16, jnp.float32
NT = (((1,), (1,)), ((), ()))
VMEM = pl.BlockSpec(memory_space=pltpu.VMEM)
SMEM = pl.BlockSpec(memory_space=pltpu.SMEM)
HBM = pl.BlockSpec(memory_space=pltpu.HBM)
MIB = 1024 * 1024
LIMITS = (16, 48, 46, 16, 16)
GROUP = 8
MAIN, TAIL_AT, TAIL_STEP, WIRE = 256, 512, 64, 640


def mm(a, b):
    return jnp.dot(a, b, preferred_element_type=F32)


def mm_nt(a, b):
    return lax.dot_general(a, b, NT, preferred_element_type=F32)


def write_hot(out, first_col, idx, base=0):
    n = idx.shape[1]
    row = lax.broadcasted_iota(jnp.int32, (16, n), 0) + base
    gap = (jnp.broadcast_to(idx, (16, n)) - row).astype(jnp.int16)
    one, zero = jnp.ones((16, n), BF), jnp.zeros((16, n), BF)
    for r in range(0, out.shape[0], 16):
        out[r : r + 16, pl.ds(first_col, n)] = jnp.where(gap == jnp.int16(r), one, zero)


def pack_wire(wire, r, blocks, prof):
    n = blocks[0].shape[1]
    tails = []
    for par, block in enumerate(blocks):
        wire[r, :, par * MAIN : (par + 1) * MAIN] = block[:MAIN].T.astype(BF)
        fill = jnp.zeros((TAIL_STEP - (prof - MAIN), n), block.dtype)
        tails.extend([block[MAIN:], fill])
    wire[r, :, TAIL_AT:] = jnp.concatenate(tails, axis=0).T.astype(BF)


def unpack_wire(wire, out, prof):
    n = wire.shape[1]
    for r in range(2):
        turned = wire[r].astype(F32).T.astype(BF)
        for par in range(2):
            c = 2 * r + par
            out[0:MAIN, c * n : (c + 1) * n] = turned[par * MAIN : (par + 1) * MAIN]
            at = TAIL_AT + par * TAIL_STEP
            out[MAIN:prof, c * n : (c + 1) * n] = turned[at : at + prof - MAIN]


def send_kernel(cols_in, plan, wire, hot, cols, sem):
    prof, n_cols = cols.shape
    copy = pltpu.make_async_copy(cols_in, cols, sem)
    copy.start()
    n = plan.shape[1]
    for c in range(4):
        write_hot(hot, c * n, plan[c : c + 1, :])
    copy.wait()
    for r in range(2):
        blocks = [mm(cols[...], hot[:, c * n : (c + 1) * n]) for c in (2 * r, 2 * r + 1)]
        pack_wire(wire, r, blocks, prof)


def edge_kernel(wire, slot, valid, dep, jac_t, arrived, first, last, deps, hot, sems):
    copies = [
        pltpu.make_async_copy(dep.at[line], deps.at[k], sems.at[k]) for k, line in enumerate((0, dep.shape[0] - 1))
    ]
    for copy in copies:
        copy.start()
    prof = arrived.shape[0]
    unpack_wire(wire, arrived, prof)
    n_pos = dep.shape[2]
    end = slot.shape[1] - n_pos
    write_hot(hot, 0, jnp.concatenate([slot[:, :n_pos], slot[:, end:]], axis=1))
    obs = mm(arrived[...], hot[...]).astype(BF)
    model = mm(jac_t[...], obs)
    for k, at, out in ((0, 0, first), (1, end, last)):
        copies[k].wait()
        res = model[:, k * n_pos : (k + 1) * n_pos] - deps[k].astype(F32)
        out[...] = jnp.where(valid[:, at : at + n_pos] > 0, res, 0.0).astype(BF)


def main_kernel(rf, inner, arrived_in, slot, valid, dep, jac_in, prec_in, part_out, edges_out, *scratch):
    arrived, jac_t, prec, deps, hot, obs_s, res_s, w_s, sc_s, part, in_sem, group_sem, out_sem = scratch
    n_slots = arrived.shape[1]
    n_lines, n_chan, n_pos = dep.shape
    total = n_lines * n_pos
    size = GROUP
    width = size * n_pos
    count = n_lines // size

    def dep_copy(g):
        span = pl.ds(g * size, size)
        return pltpu.make_async_copy(dep.at[span], deps.at[span], group_sem.at[g])

    whole = [
        pltpu.make_async_copy(src, dst, in_sem.at[k])
        for k, (src, dst) in enumerate(((arrived_in, arrived), (jac_in, jac_t), (prec_in, prec)))
    ]
    for copy in whole:
        copy.start()
    dep_copy(0).start()
    for copy in whole:
        copy.wait()

    @pl.loop(0, count)
    def _(g):
        dep_copy(g).wait()

        @pl.when(g + 1 < count)
        def _():
            dep_copy(g + 1).start()

        at = pl.multiple_of(g * width, width)
        lanes = pl.ds(at, width)
        write_hot(hot, at, slot[:, lanes])
        obs_s[...] = mm(arrived[...], hot[:, lanes]).astype(BF)
        model = mm(jac_t[...], obs_s[...])
        own = jnp.concatenate([deps[g * size + k] for k in range(size)], axis=1)
        res_s[...] = jnp.where(valid[:, lanes] > 0, model - own.astype(F32), 0.0).astype(BF)
        w_s[:, lanes] = rf * mm(prec[...], res_s[...])

    sides = [
        pltpu.make_async_copy(w_s.at[:, pl.ds(at, 2 * n_pos)], edges_out.at[:, pl.ds(to, 2 * n_pos)], out_sem.at[4 + k])
        for k, (at, to) in enumerate(((0, 0), (total - 2 * n_pos, 2 * n_pos)))
    ]
    for copy in sides:
        copy.start()

    def scale(rows):
        before, here = w_s[rows, 0:n_pos], w_s[rows, n_pos : 2 * n_pos]
        for i in range(1, n_lines - 1):
            after = w_s[rows, (i + 1) * n_pos : (i + 2) * n_pos]
            sc_s[rows, i * n_pos : (i + 1) * n_pos] = ((inner / rf) * here - (before + after)).astype(BF)
            before, here = here, after

    @pl.loop(0, n_chan // 16)
    def _(c):
        scale(pl.ds(pl.multiple_of(c * 16, 16), 16))

    if n_chan % 16:
        scale(pl.ds(n_chan // 16 * 16, n_chan % 16))

    inside = slice(n_pos, total - n_pos)
    step = n_slots // 4

    def part_copy(q):
        lanes = pl.ds(pl.multiple_of(q * step, step), step)
        return pltpu.make_async_copy(part.at[:, lanes], part_out.at[:, lanes], out_sem.at[q])

    @pl.loop(0, 4)
    def _(q):
        at = pl.multiple_of(q * step, step)
        part[:, pl.ds(at, step)] = mm_nt(sc_s[:, inside], hot[pl.ds(at, step), inside])
        part_copy(q).start()

    for copy in sides:
        copy.wait()
    for q in range(4):
        part_copy(q).wait()


def finish_kernel(rf, norm, inner, n_band, band, before, after, edges, slot, part, jac, prec, wire):
    prof = jac.shape[0]
    n_slots = part.shape[1]
    n_pos = before.shape[1]
    total = slot.shape[1]
    step = n_slots // 4
    outer = rf * mm(prec[...], jnp.concatenate([before[...], after[...]], axis=1))
    ends = []
    for side, bound in ((0, 0), (1, n_band - 1)):
        own = edges[:, 3 * side * n_pos : (3 * side + 1) * n_pos]
        inside = edges[:, (1 + side) * n_pos : (2 + side) * n_pos]
        beyond = outer[:, side * n_pos : (side + 1) * n_pos]
        ratio = jnp.where(band[0] == bound, norm / rf, inner / rf).astype(F32)
        ends.append((ratio * own - (inside + beyond)).astype(BF))
    scaled = jnp.concatenate(ends, axis=1)
    idx = jnp.concatenate([slot[:, 0:n_pos], slot[:, total - n_pos :]], axis=1)
    for r in range(2):
        blocks = []
        for c in (2 * r, 2 * r + 1):
            row = lax.broadcasted_iota(jnp.int32, (step, 2 * n_pos), 0) + c * step
            hot = jnp.where(row == idx, 1.0, 0.0).astype(BF)
            sums = part[:, c * step : (c + 1) * step] + mm_nt(scaled, hot)
            high = sums.astype(BF)
            low = (sums - high.astype(F32)).astype(BF)
            blocks.append(mm(jac[...], high) + mm(jac[...], low))
        pack_wire(wire, r, blocks, prof)


def collect_kernel(wire, plan, grad, back, hot, out, sems):
    prof = back.shape[0]
    n_steps, step = out.shape[0], out.shape[2]
    n = plan.shape[1]
    unpack_wire(wire, back, prof)
    copies = []
    for q in range(n_steps):
        for c in range(4):
            write_hot(hot.at[q], c * n, plan[c : c + 1, :], q * step)
        out[q] = mm_nt(back[...], hot[q])
        copies.append(pltpu.make_async_copy(out.at[q], grad.at[:, pl.ds(q * step, step)], sems.at[q]))
        copies[q].start()
    for copy in copies:
        copy.wait()


def call(body, outs, in_specs, limit, flops=0, scratch=(), out_specs=None):
    return pl.pallas_call(
        body,
        out_shape=outs,
        in_specs=in_specs,
        out_specs=out_specs or [VMEM] * len(outs),
        scratch_shapes=list(scratch),
        compiler_params=pltpu.CompilerParams(vmem_limit_bytes=int(limit * MIB)),
        cost_estimate=pl.CostEstimate(flops=flops, bytes_accessed=8 * MIB, transcendentals=0),
    )


def on_device(columns, departures, jacobian, chan_precision, send_rows, obs_slot, counts):
    decay = math.exp(-1.0 / corr_length)
    norm = 1.0 / (1.0 - decay * decay)
    rf, inner = decay * norm, (1.0 + decay * decay) * norm
    n_band = lax.axis_size("band")
    n_dev = n_band * lax.axis_size("lev")
    n_cols, prof = columns.shape
    _, n_lines, n_pos, n_chan = departures.shape
    total = n_lines * n_pos
    depth = send_rows.shape[2]
    n_slots = n_dev * depth
    sds = jax.ShapeDtypeStruct

    plan = send_rows[0].T
    jac_t = jacobian.T
    dep = departures[0].transpose(0, 2, 1)
    valid = jnp.arange(n_pos, dtype=jnp.int32)[None, :] < counts[0][:, None]
    slots = (obs_slot[0] % depth) * n_dev + obs_slot[0] // depth
    slots = jnp.where(valid, slots, -1).reshape(1, total)
    valid = valid.astype(jnp.int32).reshape(1, total)

    wire_shape = sds((2, n_dev, WIRE), BF)

    def exchange(wire):
        sent = wire.transpose(1, 0, 2)
        got = lax.all_to_all(sent, ("band", "lev"), split_axis=0, concat_axis=0, tiled=True)
        return got.transpose(1, 0, 2)

    dma = pltpu.SemaphoreType.DMA
    vm = pltpu.VMEM
    (wire,) = call(
        send_kernel,
        [wire_shape],
        [HBM, VMEM],
        LIMITS[0],
        2**31,
        scratch=[vm((n_cols, n_slots), BF), vm((prof, n_cols), BF), dma],
    )(columns.T, plan)
    got = exchange(wire)
    line_shape = sds((n_chan, n_pos), BF)
    arrived, first, last = call(
        edge_kernel,
        [sds((prof, n_slots), BF), line_shape, line_shape],
        [VMEM] * 3 + [HBM, VMEM],
        LIMITS[1],
        2**30,
        scratch=[vm((2, n_chan, n_pos), BF), vm((n_slots, 2 * n_pos), BF), dma((2,))],
    )(got, slots, valid, dep, jac_t)
    ends = n_band - 1
    before = lax.ppermute(last, "band", [(i, i + 1) for i in range(ends)])
    after = lax.ppermute(first, "band", [(i + 1, i) for i in range(ends)])
    part, edges = call(
        functools.partial(main_kernel, rf, inner),
        [sds((n_chan, n_slots), F32), sds((n_chan, 4 * n_pos), F32)],
        [HBM, VMEM, VMEM, HBM, HBM, HBM],
        LIMITS[2],
        2**34,
        scratch=[
            vm((prof, n_slots), BF),
            vm((n_chan, prof), BF),
            vm((n_chan, n_chan), BF),
            vm((n_lines, n_chan, n_pos), BF),
            vm((n_slots, total), BF),
            vm((prof, GROUP * n_pos), BF),
            vm((n_chan, GROUP * n_pos), BF),
            vm((n_chan, total), F32),
            vm((n_chan, total), BF),
            vm((n_chan, n_slots), F32),
            dma((3,)),
            dma((n_lines // GROUP,)),
            dma((6,)),
        ],
        out_specs=[HBM] * 2,
    )(arrived, slots, valid, dep, jac_t, chan_precision)
    band = lax.axis_index("band").reshape(1)
    (wire,) = call(
        functools.partial(finish_kernel, rf, norm, inner, n_band),
        [wire_shape],
        [SMEM] + [VMEM] * 7,
        LIMITS[3],
        2**31,
    )(band, before, after, edges, slots, part, jacobian, chan_precision)
    back = exchange(wire)
    (grad,) = call(
        collect_kernel,
        [sds((prof, n_cols), F32)],
        [VMEM, VMEM],
        LIMITS[4],
        2**31,
        scratch=[
            vm((prof, n_slots), BF),
            vm((4, n_cols // 4, n_slots), BF),
            vm((4, prof, n_cols // 4), F32),
            dma((4,)),
        ],
        out_specs=[HBM],
    )(back, plan)
    return grad.T


def solution(mesh):
    placed = (
        P(("band", "lev"), None),
        P("lev", "band", None, None),
        P(),
        P(),
        P(("band", "lev"), None, None),
        P("lev", "band", None),
        P("lev", "band"),
    )
    return jax.shard_map(
        on_device, mesh=mesh, in_specs=placed, out_specs=P(("band", "lev"), None), check_vma=False
    )
```

```python
import functools
import math

import jax
import jax.numpy as jnp
from jax import lax
from jax.experimental import pallas as pl
from jax.experimental.pallas import tpu as pltpu
from jax.sharding import PartitionSpec as P

corr_length = 2.0
BF, F32 = jnp.bfloat16, jnp.float32
NT = (((1,), (1,)), ((), ()))
VMEM = pl.BlockSpec(memory_space=pltpu.VMEM)
SMEM = pl.BlockSpec(memory_space=pltpu.SMEM)
HBM = pl.BlockSpec(memory_space=pltpu.HBM)
MIB = 1024 * 1024
LIMITS = (53, 48, 46, 16, 16)
GROUP = 8
MAIN, TAIL_AT, TAIL_STEP, WIRE = 256, 512, 64, 640


def mm(a, b):
    return jnp.dot(a, b, preferred_element_type=F32)


def mm_nt(a, b):
    return lax.dot_general(a, b, NT, preferred_element_type=F32)


def write_hot(out, first_col, idx, base=0):
    n = idx.shape[1]
    row = lax.broadcasted_iota(jnp.int32, (16, n), 0) + base
    gap = (jnp.broadcast_to(idx, (16, n)) - row).astype(jnp.int16)
    one, zero = jnp.ones((16, n), BF), jnp.zeros((16, n), BF)
    for r in range(0, out.shape[0], 16):
        out[r : r + 16, pl.ds(first_col, n)] = jnp.where(gap == jnp.int16(r), one, zero)


def pack_wire(wire, r, blocks, prof):
    n = blocks[0].shape[1]
    tails = []
    for par, block in enumerate(blocks):
        wire[r, :, par * MAIN : (par + 1) * MAIN] = block[:MAIN].T.astype(BF)
        fill = jnp.zeros((TAIL_STEP - (prof - MAIN), n), block.dtype)
        tails.extend([block[MAIN:], fill])
    wire[r, :, TAIL_AT:] = jnp.concatenate(tails, axis=0).T.astype(BF)


def unpack_wire(wire, out, prof):
    n = wire.shape[1]
    for r in range(2):
        turned = wire[r].astype(F32).T.astype(BF)
        for par in range(2):
            c = 2 * r + par
            out[0:MAIN, c * n : (c + 1) * n] = turned[par * MAIN : (par + 1) * MAIN]
            at = TAIL_AT + par * TAIL_STEP
            out[MAIN:prof, c * n : (c + 1) * n] = turned[at : at + prof - MAIN]


def send_kernel(cols_in, plan, wire, hot, cols, sem):
    prof, n_cols = cols.shape
    copy = pltpu.make_async_copy(cols_in, cols, sem)
    copy.start()
    n = plan.shape[1]
    for c in range(4):
        write_hot(hot, c * n, plan[c : c + 1, :])
    copy.wait()
    for r in range(2):
        blocks = [mm(cols[...], hot[:, c * n : (c + 1) * n]) for c in (2 * r, 2 * r + 1)]
        pack_wire(wire, r, blocks, prof)


def edge_kernel(wire, slot, valid, dep, jac_t, arrived, first, last, deps, hot, sems):
    copies = [
        pltpu.make_async_copy(dep.at[line], deps.at[k], sems.at[k]) for k, line in enumerate((0, dep.shape[0] - 1))
    ]
    for copy in copies:
        copy.start()
    prof = arrived.shape[0]
    unpack_wire(wire, arrived, prof)
    n_pos = dep.shape[2]
    end = slot.shape[1] - n_pos
    write_hot(hot, 0, jnp.concatenate([slot[:, :n_pos], slot[:, end:]], axis=1))
    obs = mm(arrived[...], hot[...]).astype(BF)
    model = mm(jac_t[...], obs)
    for k, at, out in ((0, 0, first), (1, end, last)):
        copies[k].wait()
        res = model[:, k * n_pos : (k + 1) * n_pos] - deps[k].astype(F32)
        out[...] = jnp.where(valid[:, at : at + n_pos] > 0, res, 0.0).astype(BF)


def main_kernel(rf, inner, arrived_in, slot, valid, dep, jac_in, prec_in, part_out, edges_out, *scratch):
    arrived, jac_t, prec, deps, hot, obs_s, res_s, w_s, sc_s, part, in_sem, group_sem, out_sem = scratch
    n_slots = arrived.shape[1]
    n_lines, n_chan, n_pos = dep.shape
    total = n_lines * n_pos
    size = GROUP
    width = size * n_pos
    count = n_lines // size

    def dep_copy(g):
        span = pl.ds(g * size, size)
        return pltpu.make_async_copy(dep.at[span], deps.at[span], group_sem.at[g])

    whole = [
        pltpu.make_async_copy(src, dst, in_sem.at[k])
        for k, (src, dst) in enumerate(((arrived_in, arrived), (jac_in, jac_t), (prec_in, prec)))
    ]
    for copy in whole:
        copy.start()
    dep_copy(0).start()
    for copy in whole:
        copy.wait()

    @pl.loop(0, count)
    def _(g):
        dep_copy(g).wait()

        @pl.when(g + 1 < count)
        def _():
            dep_copy(g + 1).start()

        at = pl.multiple_of(g * width, width)
        lanes = pl.ds(at, width)
        write_hot(hot, at, slot[:, lanes])
        obs_s[...] = mm(arrived[...], hot[:, lanes]).astype(BF)
        model = mm(jac_t[...], obs_s[...])
        own = jnp.concatenate([deps[g * size + k] for k in range(size)], axis=1)
        res_s[...] = jnp.where(valid[:, lanes] > 0, model - own.astype(F32), 0.0).astype(BF)
        w_s[:, lanes] = rf * mm(prec[...], res_s[...])

    sides = [
        pltpu.make_async_copy(w_s.at[:, pl.ds(at, 2 * n_pos)], edges_out.at[:, pl.ds(to, 2 * n_pos)], out_sem.at[4 + k])
        for k, (at, to) in enumerate(((0, 0), (total - 2 * n_pos, 2 * n_pos)))
    ]
    for copy in sides:
        copy.start()

    def scale(rows):
        before, here = w_s[rows, 0:n_pos], w_s[rows, n_pos : 2 * n_pos]
        for i in range(1, n_lines - 1):
            after = w_s[rows, (i + 1) * n_pos : (i + 2) * n_pos]
            sc_s[rows, i * n_pos : (i + 1) * n_pos] = ((inner / rf) * here - (before + after)).astype(BF)
            before, here = here, after

    @pl.loop(0, n_chan // 16)
    def _(c):
        scale(pl.ds(pl.multiple_of(c * 16, 16), 16))

    if n_chan % 16:
        scale(pl.ds(n_chan // 16 * 16, n_chan % 16))

    inside = slice(n_pos, total - n_pos)
    step = n_slots // 4

    def part_copy(q):
        lanes = pl.ds(pl.multiple_of(q * step, step), step)
        return pltpu.make_async_copy(part.at[:, lanes], part_out.at[:, lanes], out_sem.at[q])

    @pl.loop(0, 4)
    def _(q):
        at = pl.multiple_of(q * step, step)
        part[:, pl.ds(at, step)] = mm_nt(sc_s[:, inside], hot[pl.ds(at, step), inside])
        part_copy(q).start()

    for copy in sides:
        copy.wait()
    for q in range(4):
        part_copy(q).wait()


def finish_kernel(rf, norm, inner, n_band, band, before, after, edges, slot, part, jac, prec, wire):
    prof = jac.shape[0]
    n_slots = part.shape[1]
    n_pos = before.shape[1]
    total = slot.shape[1]
    step = n_slots // 4
    outer = rf * mm(prec[...], jnp.concatenate([before[...], after[...]], axis=1))
    ends = []
    for side, bound in ((0, 0), (1, n_band - 1)):
        own = edges[:, 3 * side * n_pos : (3 * side + 1) * n_pos]
        inside = edges[:, (1 + side) * n_pos : (2 + side) * n_pos]
        beyond = outer[:, side * n_pos : (side + 1) * n_pos]
        ratio = jnp.where(band[0] == bound, norm / rf, inner / rf).astype(F32)
        ends.append((ratio * own - (inside + beyond)).astype(BF))
    scaled = jnp.concatenate(ends, axis=1)
    idx = jnp.concatenate([slot[:, 0:n_pos], slot[:, total - n_pos :]], axis=1)
    for r in range(2):
        blocks = []
        for c in (2 * r, 2 * r + 1):
            row = lax.broadcasted_iota(jnp.int32, (step, 2 * n_pos), 0) + c * step
            hot = jnp.where(row == idx, 1.0, 0.0).astype(BF)
            sums = part[:, c * step : (c + 1) * step] + mm_nt(scaled, hot)
            high = sums.astype(BF)
            low = (sums - high.astype(F32)).astype(BF)
            blocks.append(mm(jac[...], high) + mm(jac[...], low))
        pack_wire(wire, r, blocks, prof)


def collect_kernel(wire, plan, grad, back, hot, out, sems):
    prof = back.shape[0]
    n_steps, step = out.shape[0], out.shape[2]
    n = plan.shape[1]
    unpack_wire(wire, back, prof)
    copies = []
    for q in range(n_steps):
        for c in range(4):
            write_hot(hot.at[q], c * n, plan[c : c + 1, :], q * step)
        out[q] = mm_nt(back[...], hot[q])
        copies.append(pltpu.make_async_copy(out.at[q], grad.at[:, pl.ds(q * step, step)], sems.at[q]))
        copies[q].start()
    for copy in copies:
        copy.wait()


def call(body, outs, in_specs, limit, flops=0, scratch=(), out_specs=None):
    return pl.pallas_call(
        body,
        out_shape=outs,
        in_specs=in_specs,
        out_specs=out_specs or [VMEM] * len(outs),
        scratch_shapes=list(scratch),
        compiler_params=pltpu.CompilerParams(vmem_limit_bytes=int(limit * MIB)),
        cost_estimate=pl.CostEstimate(flops=flops, bytes_accessed=8 * MIB, transcendentals=0),
    )


def on_device(columns, departures, jacobian, chan_precision, send_rows, obs_slot, counts):
    decay = math.exp(-1.0 / corr_length)
    norm = 1.0 / (1.0 - decay * decay)
    rf, inner = decay * norm, (1.0 + decay * decay) * norm
    n_band = lax.axis_size("band")
    n_dev = n_band * lax.axis_size("lev")
    n_cols, prof = columns.shape
    _, n_lines, n_pos, n_chan = departures.shape
    total = n_lines * n_pos
    depth = send_rows.shape[2]
    n_slots = n_dev * depth
    sds = jax.ShapeDtypeStruct

    plan = send_rows[0].T
    jac_t = jacobian.T
    dep = departures[0].transpose(0, 2, 1)
    valid = jnp.arange(n_pos, dtype=jnp.int32)[None, :] < counts[0][:, None]
    slots = (obs_slot[0] % depth) * n_dev + obs_slot[0] // depth
    slots = jnp.where(valid, slots, -1).reshape(1, total)
    valid = valid.astype(jnp.int32).reshape(1, total)

    wire_shape = sds((2, n_dev, WIRE), BF)

    def exchange(wire):
        sent = wire.transpose(1, 0, 2)
        got = lax.all_to_all(sent, ("band", "lev"), split_axis=0, concat_axis=0, tiled=True)
        return got.transpose(1, 0, 2)

    dma = pltpu.SemaphoreType.DMA
    vm = pltpu.VMEM
    (wire,) = call(
        send_kernel,
        [wire_shape],
        [HBM, VMEM],
        LIMITS[0],
        2**31,
        scratch=[vm((n_cols, n_slots), BF), vm((prof, n_cols), BF), dma],
    )(columns.T, plan)
    got = exchange(wire)
    line_shape = sds((n_chan, n_pos), BF)
    arrived, first, last = call(
        edge_kernel,
        [sds((prof, n_slots), BF), line_shape, line_shape],
        [VMEM] * 3 + [HBM, VMEM],
        LIMITS[1],
        2**30,
        scratch=[vm((2, n_chan, n_pos), BF), vm((n_slots, 2 * n_pos), BF), dma((2,))],
    )(got, slots, valid, dep, jac_t)
    ends = n_band - 1
    before = lax.ppermute(last, "band", [(i, i + 1) for i in range(ends)])
    after = lax.ppermute(first, "band", [(i + 1, i) for i in range(ends)])
    part, edges = call(
        functools.partial(main_kernel, rf, inner),
        [sds((n_chan, n_slots), F32), sds((n_chan, 4 * n_pos), F32)],
        [HBM, VMEM, VMEM, HBM, HBM, HBM],
        LIMITS[2],
        2**34,
        scratch=[
            vm((prof, n_slots), BF),
            vm((n_chan, prof), BF),
            vm((n_chan, n_chan), BF),
            vm((n_lines, n_chan, n_pos), BF),
            vm((n_slots, total), BF),
            vm((prof, GROUP * n_pos), BF),
            vm((n_chan, GROUP * n_pos), BF),
            vm((n_chan, total), F32),
            vm((n_chan, total), BF),
            vm((n_chan, n_slots), F32),
            dma((3,)),
            dma((n_lines // GROUP,)),
            dma((6,)),
        ],
        out_specs=[HBM] * 2,
    )(arrived, slots, valid, dep, jac_t, chan_precision)
    band = lax.axis_index("band").reshape(1)
    (wire,) = call(
        functools.partial(finish_kernel, rf, norm, inner, n_band),
        [wire_shape],
        [SMEM] + [VMEM] * 7,
        LIMITS[3],
        2**31,
    )(band, before, after, edges, slots, part, jacobian, chan_precision)
    back = exchange(wire)
    (grad,) = call(
        collect_kernel,
        [sds((prof, n_cols), F32)],
        [VMEM, VMEM],
        LIMITS[4],
        2**31,
        scratch=[
            vm((prof, n_slots), BF),
            vm((4, n_cols // 4, n_slots), BF),
            vm((4, prof, n_cols // 4), F32),
            dma((4,)),
        ],
        out_specs=[HBM],
    )(back, plan)
    return grad.T


def solution(mesh):
    placed = (
        P(("band", "lev"), None),
        P("lev", "band", None, None),
        P(),
        P(),
        P(("band", "lev"), None, None),
        P("lev", "band", None),
        P("lev", "band"),
    )
    return jax.shard_map(
        on_device, mesh=mesh, in_specs=placed, out_specs=P(("band", "lev"), None), check_vma=False
    )
```

```python
import functools
import math

import jax
import jax.numpy as jnp
from jax import lax
from jax.experimental import pallas as pl
from jax.experimental.pallas import tpu as pltpu
from jax.sharding import PartitionSpec as P

corr_length = 2.0
BF, F32 = jnp.bfloat16, jnp.float32
NT = (((1,), (1,)), ((), ()))
VMEM = pl.BlockSpec(memory_space=pltpu.VMEM)
SMEM = pl.BlockSpec(memory_space=pltpu.SMEM)
HBM = pl.BlockSpec(memory_space=pltpu.HBM)
MIB = 1024 * 1024
LIMITS = (53, 48, 46, 16, 16)
GROUP = 8
MAIN, TAIL_AT, TAIL_STEP, WIRE = 256, 512, 64, 640


def mm(a, b):
    return jnp.dot(a, b, preferred_element_type=F32)


def mm_nt(a, b):
    return lax.dot_general(a, b, NT, preferred_element_type=F32)


def write_hot(out, first_col, idx, base=0):
    n = idx.shape[1]
    row = lax.broadcasted_iota(jnp.int32, (16, n), 0) + base
    gap = (jnp.broadcast_to(idx, (16, n)) - row).astype(jnp.int16)
    one, zero = jnp.ones((16, n), BF), jnp.zeros((16, n), BF)
    for r in range(0, out.shape[0], 16):
        out[r : r + 16, pl.ds(first_col, n)] = jnp.where(gap == jnp.int16(r), one, zero)


def pack_wire(wire, r, blocks, prof):
    n = blocks[0].shape[1]
    tails = []
    for par, block in enumerate(blocks):
        wire[r, :, par * MAIN : (par + 1) * MAIN] = block[:MAIN].T.astype(BF)
        fill = jnp.zeros((TAIL_STEP - (prof - MAIN), n), block.dtype)
        tails.extend([block[MAIN:], fill])
    wire[r, :, TAIL_AT:] = jnp.concatenate(tails, axis=0).T.astype(BF)


def unpack_wire(wire, out, prof):
    n = wire.shape[1]
    for r in range(2):
        turned = wire[r].astype(F32).T.astype(BF)
        for par in range(2):
            c = 2 * r + par
            out[0:MAIN, c * n : (c + 1) * n] = turned[par * MAIN : (par + 1) * MAIN]
            at = TAIL_AT + par * TAIL_STEP
            out[MAIN:prof, c * n : (c + 1) * n] = turned[at : at + prof - MAIN]


def send_kernel(cols_in, plan, wire, hot, cols, sem):
    prof, n_cols = cols.shape
    copy = pltpu.make_async_copy(cols_in, cols, sem)
    copy.start()
    n = plan.shape[1]
    for c in range(2):
        write_hot(hot, c * n, plan[c : c + 1, :])
    copy.wait()
    for c in range(2, 4):
        write_hot(hot, c * n, plan[c : c + 1, :])
    for r in range(2):
        blocks = [mm(cols[...], hot[:, c * n : (c + 1) * n]) for c in (2 * r, 2 * r + 1)]
        pack_wire(wire, r, blocks, prof)


def edge_kernel(wire, slot, valid, dep, jac_t, arrived, first, last, deps, hot, sems):
    copies = [
        pltpu.make_async_copy(dep.at[line], deps.at[k], sems.at[k]) for k, line in enumerate((0, dep.shape[0] - 1))
    ]
    for copy in copies:
        copy.start()
    prof = arrived.shape[0]
    unpack_wire(wire, arrived, prof)
    n_pos = dep.shape[2]
    end = slot.shape[1] - n_pos
    write_hot(hot, 0, jnp.concatenate([slot[:, :n_pos], slot[:, end:]], axis=1))
    obs = mm(arrived[...], hot[...]).astype(BF)
    model = mm(jac_t[...], obs)
    for k, at, out in ((0, 0, first), (1, end, last)):
        copies[k].wait()
        res = model[:, k * n_pos : (k + 1) * n_pos] - deps[k].astype(F32)
        out[...] = jnp.where(valid[:, at : at + n_pos] > 0, res, 0.0).astype(BF)


def main_kernel(rf, inner, arrived_in, slot, valid, dep, jac_in, prec_in, part_out, edges_out, *scratch):
    arrived, jac_t, prec, deps, hot, obs_s, res_s, w_s, sc_s, part, in_sem, group_sem, out_sem = scratch
    n_slots = arrived.shape[1]
    n_lines, n_chan, n_pos = dep.shape
    total = n_lines * n_pos
    size = GROUP
    width = size * n_pos
    count = n_lines // size

    def dep_copy(g):
        span = pl.ds(g * size, size)
        return pltpu.make_async_copy(dep.at[span], deps.at[span], group_sem.at[g])

    whole = [
        pltpu.make_async_copy(src, dst, in_sem.at[k])
        for k, (src, dst) in enumerate(((arrived_in, arrived), (jac_in, jac_t), (prec_in, prec)))
    ]
    for copy in whole:
        copy.start()
    dep_copy(0).start()
    for copy in whole:
        copy.wait()

    @pl.loop(0, count)
    def _(g):
        dep_copy(g).wait()

        @pl.when(g + 1 < count)
        def _():
            dep_copy(g + 1).start()

        at = pl.multiple_of(g * width, width)
        lanes = pl.ds(at, width)
        write_hot(hot, at, slot[:, lanes])
        obs_s[...] = mm(arrived[...], hot[:, lanes]).astype(BF)
        model = mm(jac_t[...], obs_s[...])
        own = jnp.concatenate([deps[g * size + k] for k in range(size)], axis=1)
        res_s[...] = jnp.where(valid[:, lanes] > 0, model - own.astype(F32), 0.0).astype(BF)
        w_s[:, lanes] = rf * mm(prec[...], res_s[...])

    sides = [
        pltpu.make_async_copy(w_s.at[:, pl.ds(at, 2 * n_pos)], edges_out.at[:, pl.ds(to, 2 * n_pos)], out_sem.at[4 + k])
        for k, (at, to) in enumerate(((0, 0), (total - 2 * n_pos, 2 * n_pos)))
    ]
    for copy in sides:
        copy.start()

    def scale(rows):
        before, here = w_s[rows, 0:n_pos], w_s[rows, n_pos : 2 * n_pos]
        for i in range(1, n_lines - 1):
            after = w_s[rows, (i + 1) * n_pos : (i + 2) * n_pos]
            sc_s[rows, i * n_pos : (i + 1) * n_pos] = ((inner / rf) * here - (before + after)).astype(BF)
            before, here = here, after

    @pl.loop(0, n_chan // 32)
    def _(c):
        scale(pl.ds(pl.multiple_of(c * 32, 32), 16))
        scale(pl.ds(pl.multiple_of(c * 32 + 16, 16), 16))

    for at in range(n_chan // 32 * 32, n_chan, 16):
        scale(pl.ds(at, min(16, n_chan - at)))

    inside = slice(n_pos, total - n_pos)
    step = n_slots // 2

    def part_copy(q):
        lanes = pl.ds(pl.multiple_of(q * step, step), step)
        return pltpu.make_async_copy(part.at[:, lanes], part_out.at[:, lanes], out_sem.at[q])

    @pl.loop(0, 2)
    def _(q):
        at = pl.multiple_of(q * step, step)
        part[:, pl.ds(at, step)] = mm_nt(sc_s[:, inside], hot[pl.ds(at, step), inside])
        part_copy(q).start()

    for copy in sides:
        copy.wait()
    for q in range(2):
        part_copy(q).wait()


def finish_kernel(rf, norm, inner, n_band, band, before, after, edges, slot, part, jac, prec, wire):
    prof = jac.shape[0]
    n_slots = part.shape[1]
    n_pos = before.shape[1]
    total = slot.shape[1]
    step = n_slots // 4
    outer = rf * mm(prec[...], jnp.concatenate([before[...], after[...]], axis=1))
    ends = []
    for side, bound in ((0, 0), (1, n_band - 1)):
        own = edges[:, 3 * side * n_pos : (3 * side + 1) * n_pos]
        inside = edges[:, (1 + side) * n_pos : (2 + side) * n_pos]
        beyond = outer[:, side * n_pos : (side + 1) * n_pos]
        ratio = jnp.where(band[0] == bound, norm / rf, inner / rf).astype(F32)
        ends.append((ratio * own - (inside + beyond)).astype(BF))
    scaled = jnp.concatenate(ends, axis=1)
    idx = jnp.concatenate([slot[:, 0:n_pos], slot[:, total - n_pos :]], axis=1)
    for r in range(2):
        blocks = []
        for c in (2 * r, 2 * r + 1):
            row = lax.broadcasted_iota(jnp.int32, (step, 2 * n_pos), 0) + c * step
            hot = jnp.where(row == idx, 1.0, 0.0).astype(BF)
            sums = part[:, c * step : (c + 1) * step] + mm_nt(scaled, hot)
            high = sums.astype(BF)
            low = (sums - high.astype(F32)).astype(BF)
            blocks.append(mm(jac[...], high) + mm(jac[...], low))
        pack_wire(wire, r, blocks, prof)


def collect_kernel(wire, plan, grad, back, hot, out, sems):
    prof = back.shape[0]
    n_steps, step = out.shape[0], out.shape[2]
    n = plan.shape[1]
    unpack_wire(wire, back, prof)
    copies = []
    for q in range(n_steps):
        for c in range(4):
            write_hot(hot.at[q], c * n, plan[c : c + 1, :], q * step)
        out[q] = mm_nt(back[...], hot[q])
        copies.append(pltpu.make_async_copy(out.at[q], grad.at[:, pl.ds(q * step, step)], sems.at[q]))
        copies[q].start()
    for copy in copies:
        copy.wait()


def call(body, outs, in_specs, limit, flops=0, scratch=(), out_specs=None):
    return pl.pallas_call(
        body,
        out_shape=outs,
        in_specs=in_specs,
        out_specs=out_specs or [VMEM] * len(outs),
        scratch_shapes=list(scratch),
        compiler_params=pltpu.CompilerParams(vmem_limit_bytes=int(limit * MIB)),
        cost_estimate=pl.CostEstimate(flops=flops, bytes_accessed=8 * MIB, transcendentals=0),
    )


def on_device(columns, departures, jacobian, chan_precision, send_rows, obs_slot, counts):
    decay = math.exp(-1.0 / corr_length)
    norm = 1.0 / (1.0 - decay * decay)
    rf, inner = decay * norm, (1.0 + decay * decay) * norm
    n_band = lax.axis_size("band")
    n_dev = n_band * lax.axis_size("lev")
    n_cols, prof = columns.shape
    _, n_lines, n_pos, n_chan = departures.shape
    total = n_lines * n_pos
    depth = send_rows.shape[2]
    n_slots = n_dev * depth
    sds = jax.ShapeDtypeStruct

    plan = send_rows[0].T
    jac_t = jacobian.T
    dep = departures[0].transpose(0, 2, 1)
    valid = jnp.arange(n_pos, dtype=jnp.int32)[None, :] < counts[0][:, None]
    slots = (obs_slot[0] % depth) * n_dev + obs_slot[0] // depth
    slots = jnp.where(valid, slots, -1).reshape(1, total)
    valid = valid.astype(jnp.int32).reshape(1, total)

    wire_shape = sds((2, n_dev, WIRE), BF)

    def exchange(wire):
        sent = wire.transpose(1, 0, 2)
        got = lax.all_to_all(sent, ("band", "lev"), split_axis=0, concat_axis=0, tiled=True)
        return got.transpose(1, 0, 2)

    dma = pltpu.SemaphoreType.DMA
    vm = pltpu.VMEM
    (wire,) = call(
        send_kernel,
        [wire_shape],
        [HBM, VMEM],
        LIMITS[0],
        2**31,
        scratch=[vm((n_cols, n_slots), BF), vm((prof, n_cols), BF), dma],
    )(columns.T, plan)
    got = exchange(wire)
    line_shape = sds((n_chan, n_pos), BF)
    arrived, first, last = call(
        edge_kernel,
        [sds((prof, n_slots), BF), line_shape, line_shape],
        [VMEM] * 3 + [HBM, VMEM],
        LIMITS[1],
        2**30,
        scratch=[vm((2, n_chan, n_pos), BF), vm((n_slots, 2 * n_pos), BF), dma((2,))],
    )(got, slots, valid, dep, jac_t)
    ends = n_band - 1
    before = lax.ppermute(last, "band", [(i, i + 1) for i in range(ends)])
    after = lax.ppermute(first, "band", [(i + 1, i) for i in range(ends)])
    part, edges = call(
        functools.partial(main_kernel, rf, inner),
        [sds((n_chan, n_slots), F32), sds((n_chan, 4 * n_pos), F32)],
        [HBM, VMEM, VMEM, HBM, HBM, HBM],
        LIMITS[2],
        2**34,
        scratch=[
            vm((prof, n_slots), BF),
            vm((n_chan, prof), BF),
            vm((n_chan, n_chan), BF),
            vm((n_lines, n_chan, n_pos), BF),
            vm((n_slots, total), BF),
            vm((prof, GROUP * n_pos), BF),
            vm((n_chan, GROUP * n_pos), BF),
            vm((n_chan, total), F32),
            vm((n_chan, total), BF),
            vm((n_chan, n_slots), F32),
            dma((3,)),
            dma((n_lines // GROUP,)),
            dma((6,)),
        ],
        out_specs=[HBM] * 2,
    )(arrived, slots, valid, dep, jac_t, chan_precision)
    band = lax.axis_index("band").reshape(1)
    (wire,) = call(
        functools.partial(finish_kernel, rf, norm, inner, n_band),
        [wire_shape],
        [SMEM] + [VMEM] * 7,
        LIMITS[3],
        2**31,
    )(band, before, after, edges, slots, part, jacobian, chan_precision)
    back = exchange(wire)
    (grad,) = call(
        collect_kernel,
        [sds((prof, n_cols), F32)],
        [VMEM, VMEM],
        LIMITS[4],
        2**31,
        scratch=[
            vm((prof, n_slots), BF),
            vm((4, n_cols // 4, n_slots), BF),
            vm((4, prof, n_cols // 4), F32),
            dma((4,)),
        ],
        out_specs=[HBM],
    )(back, plan)
    return grad.T


def solution(mesh):
    placed = (
        P(("band", "lev"), None),
        P("lev", "band", None, None),
        P(),
        P(),
        P(("band", "lev"), None, None),
        P("lev", "band", None),
        P("lev", "band"),
    )
    return jax.shard_map(
        on_device, mesh=mesh, in_specs=placed, out_specs=P(("band", "lev"), None), check_vma=False
    )
```
